32 devices in a mesh: seqa: 4 (over y, x), seqb: 8 (over z, core).
Axes of the slice: x: 2, y: 2, z: 4, core: 2. Of those that a mesh axis runs over, the one named last changes fastest.
Arguments:
- query_rows: bfloat16 [8192, 1024], P(('seqa', 'seqb')), may hold values from -256 to 256
- key_rows: bfloat16 [8192, 1024], P(('seqa', 'seqb')), may hold values from -16 to 16
- value_rows: bfloat16 [8192, 1024], P(('seqa', 'seqb')), may hold values from -16 to 16
Outputs:
- attended: bfloat16 [8192, 1024], P(('seqa', 'seqb'))
The draws below stay inside these ranges and needn't reach their ends.
All inputs are finite; a program needn't handle non-finite values.
Results may differ from the reference program's by a relative error of at most 0.0027.
Values may be sent and summed in bfloat16 or wider, within the bound.
No kernel may reach another device: no remote copies, remote signals or barrier semaphores. Data moves between devices by JAX's collectives and lax.ppermute only.
A program may use at most 64 MiB of HBM per device.

```python
import jax
import jax.numpy as jnp
from jax import lax

HEADS = 8
HEAD_DIM = 128
TOK_DEV = 256
HALF_WIN = 256
D = 1024
TOKENS = 8192
RANGE_ONE = 2048
RANGE_TWO = 2048
RANGE_THREE = 8192


def layered_field(key, salt):
    base_key = jax.random.fold_in(key, salt)
    field = jnp.clip(jax.random.normal(jax.random.fold_in(base_key, 0), (TOKENS, D), jnp.float32), -4.0, 4.0)
    for level, factor in enumerate((4, 16, 64, 256)):
        offsets = jnp.clip(jax.random.normal(jax.random.fold_in(base_key, level + 1), (TOKENS // factor, D), jnp.float32), -4.0, 4.0)
        field = field + 0.7 * jnp.repeat(offsets, factor, axis=0)
    return field


def draw_key_rows(key, part):
    field = layered_field(key, 11)
    return field.astype(jnp.bfloat16)


def draw_value_rows(key, part):
    return layered_field(key, 31).astype(jnp.bfloat16)


def draw_query_rows(key, part):
    field = jnp.clip(jax.random.normal(jax.random.fold_in(key, 21), (TOKENS, D), jnp.float32), -4.0, 4.0)
    return field.astype(jnp.bfloat16)


def setup_inputs(seed: int = 0) -> dict:
    seeds = jax.random.split(jax.random.key(seed), 4)
    query_rows = draw_query_rows(jax.random.fold_in(seeds[3], 71), 0)
    key_rows = draw_key_rows(jax.random.fold_in(seeds[3], 71), 0)
    value_rows = draw_value_rows(jax.random.fold_in(seeds[3], 71), 0)
    return dict(query_rows=query_rows, key_rows=key_rows, value_rows=value_rows)


def pooled_means(rows):
    count = rows.shape[0] // 4
    return rows.astype(jnp.float32).reshape(count, 4, rows.shape[1]).mean(axis=1).astype(jnp.bfloat16)


def reference(query_rows, key_rows, value_rows):
    key_one = pooled_means(key_rows)
    key_two = pooled_means(key_one)
    key_three = pooled_means(key_two)
    key_four = pooled_means(key_three)
    value_one = pooled_means(value_rows)
    value_two = pooled_means(value_one)
    value_three = pooled_means(value_two)
    value_four = pooled_means(value_three)
    count_one = RANGE_ONE // 4
    count_two = RANGE_TWO // 16
    count_three = RANGE_THREE // 64
    padded_keys = jnp.pad(key_rows, ((HALF_WIN, HALF_WIN), (0, 0)))
    padded_values = jnp.pad(value_rows, ((HALF_WIN, HALF_WIN), (0, 0)))
    near_count = TOK_DEV + 2 * HALF_WIN
    score_scale = 1.0 / (HEAD_DIM ** 0.5)

    def one_block(block):
        first_row = (block * TOK_DEV).astype(jnp.int32)
        queries = lax.dynamic_slice_in_dim(query_rows, first_row, TOK_DEV, 0)
        near_keys = lax.dynamic_slice_in_dim(padded_keys, first_row, near_count, 0)
        near_values = lax.dynamic_slice_in_dim(padded_values, first_row, near_count, 0)
        start_one = ((first_row // RANGE_ONE) * count_one).astype(jnp.int32)
        start_two = ((first_row // RANGE_TWO) * count_two).astype(jnp.int32)
        start_three = ((first_row // RANGE_THREE) * count_three).astype(jnp.int32)
        keyset = jnp.concatenate([near_keys,
                                  lax.dynamic_slice_in_dim(key_one, start_one, count_one, 0),
                                  lax.dynamic_slice_in_dim(key_two, start_two, count_two, 0),
                                  lax.dynamic_slice_in_dim(key_three, start_three, count_three, 0),
                                  key_four], axis=0)
        valueset = jnp.concatenate([near_values,
                                    lax.dynamic_slice_in_dim(value_one, start_one, count_one, 0),
                                    lax.dynamic_slice_in_dim(value_two, start_two, count_two, 0),
                                    lax.dynamic_slice_in_dim(value_three, start_three, count_three, 0),
                                    value_four], axis=0)
        total_keys = keyset.shape[0]
        query_heads = queries.astype(jnp.float32).reshape(TOK_DEV, HEADS, HEAD_DIM)
        key_heads = keyset.astype(jnp.float32).reshape(total_keys, HEADS, HEAD_DIM)
        value_heads = valueset.astype(jnp.float32).reshape(total_keys, HEADS, HEAD_DIM)
        scores = jnp.einsum("thd,khd->htk", query_heads, key_heads) * score_scale
        column = jnp.arange(near_count, dtype=jnp.int32)[None, :]
        row_index = jnp.arange(TOK_DEV, dtype=jnp.int32)[:, None]
        key_position = first_row - HALF_WIN + column
        near_allowed = (column >= row_index) & (column <= row_index + 2 * HALF_WIN - 1)
        near_allowed = near_allowed & (key_position >= 0) & (key_position < TOKENS)
        far_allowed = jnp.ones((TOK_DEV, total_keys - near_count), dtype=bool)
        allowed = jnp.concatenate([near_allowed, far_allowed], axis=1)[None, :, :]
        masked = jnp.where(allowed, scores, -1e30)
        highest = jnp.max(masked, axis=2, keepdims=True)
        expo = jnp.where(allowed, jnp.exp(masked - highest), 0.0)
        denominator = jnp.sum(expo, axis=2)
        weights = expo.astype(jnp.bfloat16).astype(jnp.float32)
        mixed = jnp.einsum("htk,khd->thd", weights, value_heads)
        mixed = mixed / jnp.transpose(denominator)[:, :, None]
        return mixed.reshape(TOK_DEV, HEADS * HEAD_DIM).astype(jnp.bfloat16)

    blocks = lax.map(one_block, jnp.arange(TOKENS // TOK_DEV, dtype=jnp.int32))
    return blocks.reshape(TOKENS, HEADS * HEAD_DIM)
```

```python
import functools

import jax
import jax.numpy as jnp
from jax import lax
from jax.experimental import pallas as pl
from jax.experimental.pallas import tpu as pltpu
from jax.sharding import PartitionSpec as P

HEADS = 8
HEAD_DIM = 128
HALF_WIN = 256
POOL = 4
CHIPS_ONE = 4
COLUMNS_THREE = 4
AXES = ("seqa", "seqb")
NEG = -1e30
EXP2_SCALE = 1.4426950408889634 / HEAD_DIM**0.5
VMEM_LIMIT = 24 << 20
POOL_LIMIT = 67043328 - (7 << 18)


def pool_rows(rows):
    count = rows.shape[0]
    groups = lax.broadcasted_iota(jnp.int32, (count // POOL, count), 1) // POOL
    owner = lax.broadcasted_iota(jnp.int32, (count // POOL, count), 0)
    mean = jnp.where(groups == owner, 1.0 / POOL, 0.0).astype(jnp.bfloat16)
    return jnp.dot(mean, rows, preferred_element_type=jnp.float32).astype(jnp.bfloat16)


def pool_kernel(k_ref, v_ref, one_ref, three_ref, rows_ref, sem):
    copies = [
        pltpu.make_async_copy(rows, rows_ref.at[side], sem.at[side])
        for side, rows in enumerate((k_ref, v_ref))
    ]
    for copy in copies:
        copy.start()
    for side, copy in enumerate(copies):
        copy.wait()
        one = pool_rows(rows_ref[side])
        one_ref[side] = one
        three_ref[side] = pool_rows(pool_rows(one))


def pool_call(key_rows, value_rows):
    rows, width = key_rows.shape
    shapes = [(2, rows // POOL**level, width) for level in (1, 3)]
    return pl.pallas_call(
        pool_kernel,
        in_specs=[pl.BlockSpec(memory_space=pltpu.HBM)] * 2,
        out_specs=[pl.BlockSpec(memory_space=pltpu.VMEM)] * 2,
        out_shape=[jax.ShapeDtypeStruct(shape, jnp.bfloat16) for shape in shapes],
        scratch_shapes=[
            pltpu.VMEM((2, rows, width), jnp.bfloat16),
            pltpu.SemaphoreType.DMA((2,)),
        ],
        name="pool_own",
        compiler_params=pltpu.CompilerParams(vmem_limit_bytes=POOL_LIMIT),
        cost_estimate=pl.CostEstimate(
            flops=4 * rows * rows * width // POOL, bytes_accessed=5 * rows * width, transcendentals=0
        ),
    )(key_rows, value_rows)


def lift_kernel(three_ref, other_ref, next_ref, far_ref, out_ref):
    count = three_ref.shape[1]
    for side in range(2):
        out_ref[side, pl.ds(0, count), :] = three_ref[side]
        out_ref[side, pl.ds(count, count), :] = other_ref[side]
        for slot, ref in enumerate((next_ref, far_ref)):
            out_ref[side, pl.ds((2 + slot) * count, count), :] = pool_rows(pool_rows(ref[side]))


def lift_call(own_three, other_three, one_next, one_far):
    _, count, width = own_three.shape
    return pl.pallas_call(
        lift_kernel,
        in_specs=[pl.BlockSpec(memory_space=pltpu.VMEM)] * 4,
        out_specs=pl.BlockSpec(memory_space=pltpu.VMEM),
        out_shape=jax.ShapeDtypeStruct((2, 4 * count, width), jnp.bfloat16),
        name="lift",
        compiler_params=pltpu.CompilerParams(vmem_limit_bytes=VMEM_LIMIT),
        cost_estimate=pl.CostEstimate(
            flops=16 * 64 * 16 * width, bytes_accessed=1200 * width, transcendentals=0
        ),
    )(own_three, other_three, one_next, one_far)


def triangle(shape, below):
    column = lax.broadcasted_iota(jnp.int32, shape, 0)
    row = lax.broadcasted_iota(jnp.int32, shape, 1)
    gap = column - row
    return jnp.where(jnp.where(below, gap, -1 - gap) < 0, 0.0, NEG)


def key_scores(keys, queries):
    return EXP2_SCALE * lax.dot_general(
        keys, queries, (((1,), (1,)), ((), ())), preferred_element_type=jnp.float32
    )


def stage_kernel(plan, first, *refs):
    refs = list(refs)
    flags_ref = refs.pop(0)
    q_ref = refs.pop(0)
    inputs = [refs.pop(0) for _, count in plan for _ in range(count)]
    if not first:
        top_in, sum_in, acc_in = refs.pop(0), refs.pop(0), refs.pop(0)
    top_out, sum_out, acc_out = refs.pop(0), refs.pop(0), refs.pop(0)
    expo_out = refs.pop(0) if any(kind == "across" for kind, _ in plan) else None
    far_ref = refs.pop(0)
    bias_ref = refs.pop(0)
    tok = q_ref.shape[0]
    lower_core = flags_ref[0] == 0
    middle = flags_ref[2] != 0
    whole = []
    place = 0
    for kind, count in plan:
        parts = [inputs.pop(0) for _ in range(count)]
        if kind in ("own", "partner", "across"):
            whole.append((parts, kind))
        if kind == "partner":
            bias_ref[...] = triangle((tok, tok), lower_core)
        if kind == "across":
            valid = jnp.where(flags_ref[1] != 0, 0.0, NEG)
            bias_ref[...] = triangle((tok, tok), jnp.logical_not(lower_core)) + valid
        if kind in ("own", "across"):
            continue
        for side in range(2):
            at = place
            if kind == "partner":
                rows = pool_rows(parts[side][...])
            elif kind == "pick":
                rows = jnp.where(middle, parts[0][side], parts[1][side])
            else:
                rows = parts[0][side]
            far_ref[side, pl.ds(at, rows.shape[0]), :] = rows
            at += rows.shape[0]
            if kind != "far":
                lower = pool_rows(rows)
                far_ref[side, pl.ds(at, lower.shape[0]), :] = lower
                at += lower.shape[0]
        place = at
    cols = [pl.ds(head * HEAD_DIM, HEAD_DIM) for head in range(HEADS)]
    scores = []
    for head in range(HEADS):
        query = q_ref[:, cols[head]]
        pieces = []
        for parts, kind in whole:
            piece = key_scores(parts[0][:, cols[head]], query)
            pieces.append(piece if kind == "own" else piece + bias_ref[...])
        pieces.append(key_scores(far_ref[0, pl.ds(0, place), cols[head]], query))
        scores.append(pieces)
    highest, keep = [], []
    for head in range(HEADS):
        top = functools.reduce(
            jnp.maximum, [jnp.max(piece, axis=0, keepdims=True) for piece in scores[head]]
        )
        if not first:
            before = top_in[pl.ds(head, 1), :]
            top = jnp.maximum(top, before)
            keep.append(jnp.exp2(before - top))
        highest.append(top)
    expos, totals = [], []
    for head in range(HEADS):
        expos.append([jnp.exp2(piece - highest[head]) for piece in scores[head]])
        total = sum(jnp.sum(piece, axis=0, keepdims=True) for piece in expos[head])
        if not first:
            total = total + sum_in[pl.ds(head, 1), :] * keep[head]
        totals.append(total)
    for head in range(HEADS):
        mixed = 0.0
        for (parts, kind), expo in zip(whole, expos[head]):
            if kind == "across":
                expo_out[pl.ds(head * tok, tok), :] = expo.astype(jnp.bfloat16)
            else:
                mixed = mixed + weighted(parts[1][:, cols[head]], expo.astype(jnp.bfloat16))
        mixed = mixed + weighted(
            far_ref[1, pl.ds(0, place), cols[head]], expos[head][-1].astype(jnp.bfloat16)
        )
        if not first:
            mixed = mixed + acc_in[cols[head], :] * keep[head]
        acc_out[cols[head], :] = mixed
        top_out[pl.ds(head, 1), :] = highest[head]
        sum_out[pl.ds(head, 1), :] = totals[head]


def weighted(values, expo):
    return lax.dot_general(
        values, expo, (((0,), (0,)), ((), ())), preferred_element_type=jnp.float32
    )


def far_count(kind, parts):
    if kind in ("own", "across"):
        return 0
    if kind == "partner":
        rows = parts[0].shape[0] // POOL
    else:
        rows = parts[0].shape[1]
    return rows if kind == "far" else rows + rows // POOL


def stage(flags, queries, inputs, state=None):
    tok, width = queries.shape
    plan = [(kind, len(arrays)) for kind, *arrays in inputs]
    arrays = [array for _, *group in inputs for array in group]
    far = sum(far_count(kind, group) for kind, *group in inputs)
    near = tok * sum(kind in ("own", "partner", "across") for kind, *_ in inputs)
    vmem = pl.BlockSpec(memory_space=pltpu.VMEM)
    operands = [flags, queries, *arrays, *(state or ())]
    stat = jax.ShapeDtypeStruct((HEADS, tok), jnp.float32)
    out_shape = [stat, stat, jax.ShapeDtypeStruct((width, tok), jnp.float32)]
    if any(kind == "across" for kind, _ in plan):
        out_shape.append(jax.ShapeDtypeStruct((HEADS * tok, tok), jnp.bfloat16))
    return pl.pallas_call(
        functools.partial(stage_kernel, plan, state is None),
        out_shape=out_shape,
        in_specs=[pl.BlockSpec(memory_space=pltpu.SMEM)] + [vmem] * (len(operands) - 1),
        out_specs=[vmem] * len(out_shape),
        scratch_shapes=[
            pltpu.VMEM((2, far, width), jnp.bfloat16),
            pltpu.VMEM((tok, tok), jnp.float32),
        ],
        compiler_params=pltpu.CompilerParams(vmem_limit_bytes=VMEM_LIMIT),
        cost_estimate=pl.CostEstimate(
            flops=4 * tok * width * (far + near),
            bytes_accessed=sum(a.size * a.dtype.itemsize for a in operands),
            transcendentals=tok * HEADS * (far + near),
        ),
    )(*operands)


def finish_kernel(value_ref, expo_ref, sum_ref, acc_ref, out_ref):
    tok = out_ref.shape[0]
    for head in range(HEADS):
        cols = pl.ds(head * HEAD_DIM, HEAD_DIM)
        mixed = weighted(value_ref[:, cols], expo_ref[pl.ds(head * tok, tok), :]) + acc_ref[cols, :]
        mixed = mixed * (1.0 / sum_ref[pl.ds(head, 1), :])
        out_ref[:, cols] = mixed.T.astype(jnp.bfloat16)


def finish(values, expo, total, mixed):
    tok, width = values.shape
    return pl.pallas_call(
        finish_kernel,
        out_shape=jax.ShapeDtypeStruct((tok, width), jnp.bfloat16),
        in_specs=[pl.BlockSpec(memory_space=pltpu.VMEM)] * 4,
        out_specs=pl.BlockSpec(memory_space=pltpu.VMEM),
        name="finish",
        compiler_params=pltpu.CompilerParams(vmem_limit_bytes=VMEM_LIMIT),
        cost_estimate=pl.CostEstimate(
            flops=2 * tok * tok * width, bytes_accessed=10 * tok * width, transcendentals=0
        ),
    )(values, expo, total, mixed)


def swap(x, axis, mask):
    return lax.ppermute(x, axis, [(i, i ^ mask) for i in range(lax.axis_size(axis))])


def spread(x, axis, low, high):
    while low < high:
        x = jnp.concatenate([x, swap(x, axis, low)], axis=1)
        low *= 2
    return x


def pooled_means(stacked):
    count = stacked.shape[1] // POOL
    split = stacked.astype(jnp.float32).reshape(2, count, POOL, stacked.shape[2])
    return split.mean(axis=2).astype(jnp.bfloat16)


def attend(query_rows, key_rows, value_rows):
    tok = query_rows.shape[0]
    assert tok == HALF_WIN
    wide, tall = lax.axis_size("seqb"), lax.axis_size("seqa")
    count = tall * wide
    group = 2 * CHIPS_ONE
    inner = lax.axis_index("seqb")
    place = lax.axis_index("seqa") * wide + inner
    core = inner & 1
    valid = jnp.where(core == 0, place > 0, place < count - 1)
    chip = (inner >> 1) & (CHIPS_ONE - 1)
    middle = (chip == 1) | (chip == 2)
    flags = jnp.stack([flag.astype(jnp.int32) for flag in (core, valid, middle)])
    bounds = [(i, i + 1) for i in range(1, count - 1, 2)]
    bounds += [(j, i) for i, j in bounds]
    own_one, own_three = pool_call(key_rows, value_rows)

    one_far = swap(own_one, "seqb", group - 2)
    one_next = swap(own_one, "seqb", 2)
    other_three = swap(own_three, "seqb", 4)
    chips = [(i, i // 2 % CHIPS_ONE) for i in range(wide)]
    one_end = lax.ppermute(own_one, "seqb", [(i, i ^ 4) for i, chip in chips if chip in (0, 3)])
    across_keys = lax.ppermute(key_rows, AXES, bounds)
    across_values = lax.ppermute(value_rows, AXES, bounds)
    partner = [swap(key_rows, "seqb", 1), swap(value_rows, "seqb", 1)]
    near_plan = [("own", key_rows, value_rows), ("one", own_one), ("partner", *partner)]
    state = stage(flags, query_rows, near_plan)
    one_mid = lax.ppermute(one_far, "seqb", [(i, i ^ 2) for i, chip in chips if chip in (1, 2)])
    three = lift_call(own_three, other_three, one_next, one_far)
    three = spread(three, "seqb", group, wide)
    three = spread(three, "seqa", 1, COLUMNS_THREE)
    far = [
        ("one", one_next),
        ("one", swap(one_next, "seqb", 1)),
        ("one", one_far),
        ("one", swap(one_far, "seqb", 1)),
    ]
    state = stage(flags, query_rows, far, state)
    wider = [
        ("pick", one_end, one_mid),
        ("pick", swap(one_end, "seqb", 1), swap(one_mid, "seqb", 1)),
        ("three", three),
        ("three", swap(three, "seqb", 1)),
    ]
    if wide > group:
        two = pooled_means(own_one)
        others = spread(two, "seqb", group, wide)[:, two.shape[1] :]
        wider.append(("far", spread(others, "seqb", 1, group)))
    if tall > COLUMNS_THREE:
        four = pooled_means(own_three)
        others = spread(four, "seqa", COLUMNS_THREE, tall)[:, four.shape[1] :]
        others = spread(others, "seqa", 1, COLUMNS_THREE)
        wider.append(("far", spread(others, "seqb", 1, wide)))
    _, total, mixed, expo = stage(flags, query_rows, wider + [("across", across_keys)], state)
    return finish(across_values, expo, total, mixed)


def solution(mesh):
    return jax.shard_map(
        attend,
        mesh=mesh,
        in_specs=(P(AXES, None), P(AXES, None), P(AXES, None)),
        out_specs=P(AXES, None),
        check_vma=False,
    )
```

```python
import functools

import jax
import jax.numpy as jnp
from jax import lax
from jax.experimental import pallas as pl
from jax.experimental.pallas import tpu as pltpu
from jax.sharding import PartitionSpec as P

HEADS = 8
HEAD_DIM = 128
HALF_WIN = 256
POOL = 4
CHIPS_ONE = 4
COLUMNS_THREE = 4
AXES = ("seqa", "seqb")
NEG = -1e30
EXP2_SCALE = 1.4426950408889634 / HEAD_DIM**0.5
VMEM_LIMIT = 24 << 20
POOL_LIMIT = 24 << 20
POOL_PARTS = 1
OUT_PARTS = 2


def pool_rows(rows):
    count = rows.shape[0]
    groups = lax.broadcasted_iota(jnp.int32, (count // POOL, count), 1) // POOL
    owner = lax.broadcasted_iota(jnp.int32, (count // POOL, count), 0)
    mean = jnp.where(groups == owner, 1.0 / POOL, 0.0).astype(jnp.bfloat16)
    return jnp.dot(mean, rows, preferred_element_type=jnp.float32).astype(jnp.bfloat16)


def pool_kernel(k_ref, v_ref, one_ref, three_ref, rows_ref, sem):
    part = rows_ref.shape[1] // POOL_PARTS
    copies = {}
    for at in range(POOL_PARTS):
        for side, ref in enumerate((k_ref, v_ref)):
            rows = pl.ds(at * part, part)
            copies[at, side] = pltpu.make_async_copy(
                ref.at[rows, :], rows_ref.at[side, rows, :], sem.at[at, side]
            )
            copies[at, side].start()
    for (at, side), copy in copies.items():
        copy.wait()
        one = pool_rows(rows_ref[side, pl.ds(at * part, part), :])
        one_ref[side, pl.ds(at * part // POOL, part // POOL), :] = one
    for side in range(2):
        three_ref[side] = pool_rows(pool_rows(one_ref[side]))


def pool_call(key_rows, value_rows):
    rows, width = key_rows.shape
    shapes = [(2, rows // POOL**level, width) for level in (1, 3)]
    return pl.pallas_call(
        pool_kernel,
        in_specs=[pl.BlockSpec(memory_space=pltpu.HBM)] * 2,
        out_specs=[pl.BlockSpec(memory_space=pltpu.VMEM)] * 2,
        out_shape=[jax.ShapeDtypeStruct(shape, jnp.bfloat16) for shape in shapes],
        scratch_shapes=[
            pltpu.VMEM((2, rows, width), jnp.bfloat16),
            pltpu.SemaphoreType.DMA((POOL_PARTS, 2)),
        ],
        name="pool_own",
        compiler_params=pltpu.CompilerParams(vmem_limit_bytes=POOL_LIMIT),
        cost_estimate=pl.CostEstimate(
            flops=4 * rows * rows * width // POOL, bytes_accessed=5 * rows * width, transcendentals=0
        ),
    )(key_rows, value_rows)


def lift_kernel(three_ref, other_ref, next_ref, far_ref, out_ref):
    count = three_ref.shape[1]
    for side in range(2):
        out_ref[side, pl.ds(0, count), :] = three_ref[side]
        out_ref[side, pl.ds(count, count), :] = other_ref[side]
        for slot, ref in enumerate((next_ref, far_ref)):
            out_ref[side, pl.ds((2 + slot) * count, count), :] = pool_rows(pool_rows(ref[side]))


def lift_call(own_three, other_three, one_next, one_far):
    _, count, width = own_three.shape
    return pl.pallas_call(
        lift_kernel,
        in_specs=[pl.BlockSpec(memory_space=pltpu.VMEM)] * 4,
        out_specs=pl.BlockSpec(memory_space=pltpu.VMEM),
        out_shape=jax.ShapeDtypeStruct((2, 4 * count, width), jnp.bfloat16),
        name="lift",
        compiler_params=pltpu.CompilerParams(vmem_limit_bytes=VMEM_LIMIT),
        cost_estimate=pl.CostEstimate(
            flops=16 * 64 * 16 * width, bytes_accessed=1200 * width, transcendentals=0
        ),
    )(own_three, other_three, one_next, one_far)


def triangle(shape, below):
    column = lax.broadcasted_iota(jnp.int32, shape, 0)
    row = lax.broadcasted_iota(jnp.int32, shape, 1)
    gap = column - row
    return jnp.where(jnp.where(below, gap, -1 - gap) < 0, 0.0, NEG)


def key_scores(keys, queries):
    return EXP2_SCALE * lax.dot_general(
        keys, queries, (((1,), (1,)), ((), ())), preferred_element_type=jnp.float32
    )


def stage_kernel(plan, first, *refs):
    refs = list(refs)
    flags_ref = refs.pop(0)
    q_ref = refs.pop(0)
    inputs = [refs.pop(0) for _, count in plan for _ in range(count)]
    if not first:
        top_in, sum_in, acc_in = refs.pop(0), refs.pop(0), refs.pop(0)
    top_out, sum_out, acc_out = refs.pop(0), refs.pop(0), refs.pop(0)
    expo_out = refs.pop(0) if any(kind == "across" for kind, _ in plan) else None
    far_ref = refs.pop(0)
    bias_ref = refs.pop(0)
    tok = q_ref.shape[0]
    lower_core = flags_ref[0] == 0
    middle = flags_ref[2] != 0
    whole = []
    place = 0
    for kind, count in plan:
        parts = [inputs.pop(0) for _ in range(count)]
        if kind in ("own", "partner", "across"):
            whole.append((parts, kind))
        if kind == "partner":
            bias_ref[...] = triangle((tok, tok), lower_core)
        if kind == "across":
            valid = jnp.where(flags_ref[1] != 0, 0.0, NEG)
            bias_ref[...] = triangle((tok, tok), jnp.logical_not(lower_core)) + valid
        if kind in ("own", "across"):
            continue
        for side in range(2):
            at = place
            if kind == "partner":
                rows = pool_rows(parts[side][...])
            elif kind == "pick":
                rows = jnp.where(middle, parts[0][side], parts[1][side])
            else:
                rows = parts[0][side]
            far_ref[side, pl.ds(at, rows.shape[0]), :] = rows
            at += rows.shape[0]
            if kind != "far":
                lower = pool_rows(rows)
                far_ref[side, pl.ds(at, lower.shape[0]), :] = lower
                at += lower.shape[0]
        place = at
    cols = [pl.ds(head * HEAD_DIM, HEAD_DIM) for head in range(HEADS)]
    scores = []
    for head in range(HEADS):
        query = q_ref[:, cols[head]]
        pieces = []
        for parts, kind in whole:
            piece = key_scores(parts[0][:, cols[head]], query)
            pieces.append(piece if kind == "own" else piece + bias_ref[...])
        pieces.append(key_scores(far_ref[0, pl.ds(0, place), cols[head]], query))
        scores.append(pieces)
    highest, keep = [], []
    for head in range(HEADS):
        top = functools.reduce(
            jnp.maximum, [jnp.max(piece, axis=0, keepdims=True) for piece in scores[head]]
        )
        if not first:
            before = top_in[pl.ds(head, 1), :]
            top = jnp.maximum(top, before)
            keep.append(jnp.exp2(before - top))
        highest.append(top)
    expos, totals = [], []
    for head in range(HEADS):
        expos.append([jnp.exp2(piece - highest[head]) for piece in scores[head]])
        total = sum(jnp.sum(piece, axis=0, keepdims=True) for piece in expos[head])
        if not first:
            total = total + sum_in[pl.ds(head, 1), :] * keep[head]
        totals.append(total)
    for head in range(HEADS):
        mixed = 0.0
        for (parts, kind), expo in zip(whole, expos[head]):
            if kind == "across":
                expo_out[pl.ds(head * tok, tok), :] = expo.astype(jnp.bfloat16)
            else:
                mixed = mixed + weighted(parts[1][:, cols[head]], expo.astype(jnp.bfloat16))
        mixed = mixed + weighted(
            far_ref[1, pl.ds(0, place), cols[head]], expos[head][-1].astype(jnp.bfloat16)
        )
        if not first:
            mixed = mixed + acc_in[cols[head], :] * keep[head]
        acc_out[cols[head], :] = mixed
        top_out[pl.ds(head, 1), :] = highest[head]
        sum_out[pl.ds(head, 1), :] = totals[head]


def weighted(values, expo):
    return lax.dot_general(
        values, expo, (((0,), (0,)), ((), ())), preferred_element_type=jnp.float32
    )


def far_count(kind, parts):
    if kind in ("own", "across"):
        return 0
    if kind == "partner":
        rows = parts[0].shape[0] // POOL
    else:
        rows = parts[0].shape[1]
    return rows if kind == "far" else rows + rows // POOL


def stage(flags, queries, inputs, state=None):
    tok, width = queries.shape
    plan = [(kind, len(arrays)) for kind, *arrays in inputs]
    arrays = [array for _, *group in inputs for array in group]
    far = sum(far_count(kind, group) for kind, *group in inputs)
    near = tok * sum(kind in ("own", "partner", "across") for kind, *_ in inputs)
    vmem = pl.BlockSpec(memory_space=pltpu.VMEM)
    operands = [flags, queries, *arrays, *(state or ())]
    stat = jax.ShapeDtypeStruct((HEADS, tok), jnp.float32)
    out_shape = [stat, stat, jax.ShapeDtypeStruct((width, tok), jnp.float32)]
    if any(kind == "across" for kind, _ in plan):
        out_shape.append(jax.ShapeDtypeStruct((HEADS * tok, tok), jnp.bfloat16))
    return pl.pallas_call(
        functools.partial(stage_kernel, plan, state is None),
        out_shape=out_shape,
        in_specs=[pl.BlockSpec(memory_space=pltpu.SMEM)] + [vmem] * (len(operands) - 1),
        out_specs=[vmem] * len(out_shape),
        scratch_shapes=[
            pltpu.VMEM((2, far, width), jnp.bfloat16),
            pltpu.VMEM((tok, tok), jnp.float32),
        ],
        compiler_params=pltpu.CompilerParams(vmem_limit_bytes=VMEM_LIMIT),
        cost_estimate=pl.CostEstimate(
            flops=4 * tok * width * (far + near),
            bytes_accessed=sum(a.size * a.dtype.itemsize for a in operands),
            transcendentals=tok * HEADS * (far + near),
        ),
    )(*operands)


def finish_kernel(value_ref, expo_ref, sum_ref, acc_ref, out_ref, rows_ref, sem):
    tok = rows_ref.shape[0]
    width = rows_ref.shape[1] // OUT_PARTS
    copies = []
    for head in range(HEADS):
        cols = pl.ds(head * HEAD_DIM, HEAD_DIM)
        mixed = weighted(value_ref[:, cols], expo_ref[pl.ds(head * tok, tok), :]) + acc_ref[cols, :]
        mixed = mixed * (1.0 / sum_ref[pl.ds(head, 1), :])
        rows_ref[:, cols] = mixed.T.astype(jnp.bfloat16)
        if (head + 1) * OUT_PARTS % HEADS == 0:
            part = (head + 1) * OUT_PARTS // HEADS - 1
            done = pl.ds(part * width, width)
            copies.append(
                pltpu.make_async_copy(rows_ref.at[:, done], out_ref.at[:, done], sem.at[part])
            )
            copies[-1].start()
    for copy in copies:
        copy.wait()


def finish(values, expo, total, mixed):
    tok, width = values.shape
    return pl.pallas_call(
        finish_kernel,
        out_shape=jax.ShapeDtypeStruct((tok, width), jnp.bfloat16),
        in_specs=[pl.BlockSpec(memory_space=pltpu.VMEM)] * 4,
        out_specs=pl.BlockSpec(memory_space=pltpu.HBM),
        scratch_shapes=[
            pltpu.VMEM((tok, width), jnp.bfloat16),
            pltpu.SemaphoreType.DMA((OUT_PARTS,)),
        ],
        name="finish",
        compiler_params=pltpu.CompilerParams(vmem_limit_bytes=VMEM_LIMIT),
        cost_estimate=pl.CostEstimate(
            flops=2 * tok * tok * width, bytes_accessed=10 * tok * width, transcendentals=0
        ),
    )(values, expo, total, mixed)


def swap(x, axis, mask):
    return lax.ppermute(x, axis, [(i, i ^ mask) for i in range(lax.axis_size(axis))])


def spread(x, axis, low, high):
    while low < high:
        x = jnp.concatenate([x, swap(x, axis, low)], axis=1)
        low *= 2
    return x


def pooled_means(stacked):
    count = stacked.shape[1] // POOL
    split = stacked.astype(jnp.float32).reshape(2, count, POOL, stacked.shape[2])
    return split.mean(axis=2).astype(jnp.bfloat16)


def attend(query_rows, key_rows, value_rows):
    tok = query_rows.shape[0]
    assert tok == HALF_WIN
    wide, tall = lax.axis_size("seqb"), lax.axis_size("seqa")
    count = tall * wide
    group = 2 * CHIPS_ONE
    inner = lax.axis_index("seqb")
    place = lax.axis_index("seqa") * wide + inner
    core = inner & 1
    valid = jnp.where(core == 0, place > 0, place < count - 1)
    chip = (inner >> 1) & (CHIPS_ONE - 1)
    middle = (chip == 1) | (chip == 2)
    flags = jnp.stack([flag.astype(jnp.int32) for flag in (core, valid, middle)])
    bounds = [(i, i + 1) for i in range(1, count - 1, 2)]
    bounds += [(j, i) for i, j in bounds]
    own_one, own_three = pool_call(key_rows, value_rows)

    one_far = swap(own_one, "seqb", group - 2)
    one_next = swap(own_one, "seqb", 2)
    other_three = swap(own_three, "seqb", 4)
    chips = [(i, i // 2 % CHIPS_ONE) for i in range(wide)]
    one_end = lax.ppermute(own_one, "seqb", [(i, i ^ 4) for i, chip in chips if chip in (0, 3)])
    across_keys = lax.ppermute(key_rows, AXES, bounds)
    across_values = lax.ppermute(value_rows, AXES, bounds)
    partner = [swap(key_rows, "seqb", 1), swap(value_rows, "seqb", 1)]
    near_plan = [("own", key_rows, value_rows), ("one", own_one), ("partner", *partner)]
    state = stage(flags, query_rows, near_plan)
    one_mid = lax.ppermute(one_far, "seqb", [(i, i ^ 2) for i, chip in chips if chip in (1, 2)])
    three = lift_call(own_three, other_three, one_next, one_far)
    three = spread(three, "seqb", group, wide)
    three = spread(three, "seqa", 1, COLUMNS_THREE)
    far = [
        ("one", one_next),
        ("one", swap(one_next, "seqb", 1)),
        ("one", one_far),
        ("one", swap(one_far, "seqb", 1)),
    ]
    state = stage(flags, query_rows, far, state)
    wider = [
        ("pick", one_end, one_mid),
        ("pick", swap(one_end, "seqb", 1), swap(one_mid, "seqb", 1)),
        ("three", three),
        ("three", swap(three, "seqb", 1)),
    ]
    if wide > group:
        two = pooled_means(own_one)
        others = spread(two, "seqb", group, wide)[:, two.shape[1] :]
        wider.append(("far", spread(others, "seqb", 1, group)))
    if tall > COLUMNS_THREE:
        four = pooled_means(own_three)
        others = spread(four, "seqa", COLUMNS_THREE, tall)[:, four.shape[1] :]
        others = spread(others, "seqa", 1, COLUMNS_THREE)
        wider.append(("far", spread(others, "seqb", 1, wide)))
    _, total, mixed, expo = stage(flags, query_rows, wider + [("across", across_keys)], state)
    return finish(across_values, expo, total, mixed)


def solution(mesh):
    return jax.shard_map(
        attend,
        mesh=mesh,
        in_specs=(P(AXES, None), P(AXES, None), P(AXES, None)),
        out_specs=P(AXES, None),
        check_vma=False,
    )
```

```python
import functools

import jax
import jax.numpy as jnp
from jax import lax
from jax.experimental import pallas as pl
from jax.experimental.pallas import tpu as pltpu
from jax.sharding import PartitionSpec as P

HEADS = 8
HEAD_DIM = 128
HALF_WIN = 256
POOL = 4
CHIPS_ONE = 4
COLUMNS_THREE = 4
AXES = ("seqa", "seqb")
NEG = -1e30
EXP2_SCALE = 1.4426950408889634 / HEAD_DIM**0.5
VMEM_LIMIT = 24 << 20
POOL_LIMIT = 24 << 20
POOL_PARTS = 1
OUT_PARTS = 2


def pool_rows(rows):
    count = rows.shape[0]
    groups = lax.broadcasted_iota(jnp.int32, (count // POOL, count), 1) // POOL
    owner = lax.broadcasted_iota(jnp.int32, (count // POOL, count), 0)
    mean = jnp.where(groups == owner, 1.0 / POOL, 0.0).astype(jnp.bfloat16)
    return jnp.dot(mean, rows, preferred_element_type=jnp.float32).astype(jnp.bfloat16)


def pool_kernel(k_ref, v_ref, one_ref, three_ref, rows_ref, sem):
    part = rows_ref.shape[1] // POOL_PARTS
    copies = {}
    for at in range(POOL_PARTS):
        for side, ref in enumerate((k_ref, v_ref)):
            rows = pl.ds(at * part, part)
            copies[at, side] = pltpu.make_async_copy(
                ref.at[rows, :], rows_ref.at[side, rows, :], sem.at[at, side]
            )
            copies[at, side].start()
    for (at, side), copy in copies.items():
        copy.wait()
        one = pool_rows(rows_ref[side, pl.ds(at * part, part), :])
        one_ref[side, pl.ds(at * part // POOL, part // POOL), :] = one
    for side in range(2):
        three_ref[side] = pool_rows(pool_rows(one_ref[side]))


def pool_call(key_rows, value_rows):
    rows, width = key_rows.shape
    shapes = [(2, rows // POOL**level, width) for level in (1, 3)]
    return pl.pallas_call(
        pool_kernel,
        in_specs=[pl.BlockSpec(memory_space=pltpu.HBM)] * 2,
        out_specs=[pl.BlockSpec(memory_space=pltpu.VMEM)] * 2,
        out_shape=[jax.ShapeDtypeStruct(shape, jnp.bfloat16) for shape in shapes],
        scratch_shapes=[
            pltpu.VMEM((2, rows, width), jnp.bfloat16),
            pltpu.SemaphoreType.DMA((POOL_PARTS, 2)),
        ],
        name="pool_own",
        compiler_params=pltpu.CompilerParams(vmem_limit_bytes=POOL_LIMIT),
        cost_estimate=pl.CostEstimate(
            flops=4 * rows * rows * width // POOL, bytes_accessed=5 * rows * width, transcendentals=0
        ),
    )(key_rows, value_rows)


def lift_kernel(three_ref, other_ref, next_ref, far_ref, out_ref):
    count = three_ref.shape[1]
    for side in range(2):
        out_ref[side, pl.ds(0, count), :] = three_ref[side]
        out_ref[side, pl.ds(count, count), :] = other_ref[side]
        for slot, ref in enumerate((next_ref, far_ref)):
            out_ref[side, pl.ds((2 + slot) * count, count), :] = pool_rows(pool_rows(ref[side]))


def lift_call(own_three, other_three, one_next, one_far):
    _, count, width = own_three.shape
    return pl.pallas_call(
        lift_kernel,
        in_specs=[pl.BlockSpec(memory_space=pltpu.VMEM)] * 4,
        out_specs=pl.BlockSpec(memory_space=pltpu.VMEM),
        out_shape=jax.ShapeDtypeStruct((2, 4 * count, width), jnp.bfloat16),
        name="lift",
        compiler_params=pltpu.CompilerParams(vmem_limit_bytes=VMEM_LIMIT),
        cost_estimate=pl.CostEstimate(
            flops=16 * 64 * 16 * width, bytes_accessed=1200 * width, transcendentals=0
        ),
    )(own_three, other_three, one_next, one_far)


def triangle(shape, below):
    column = lax.broadcasted_iota(jnp.int32, shape, 0)
    row = lax.broadcasted_iota(jnp.int32, shape, 1)
    gap = column - row
    return jnp.where(jnp.where(below, gap, -1 - gap) < 0, 0.0, NEG)


def key_scores(keys, queries):
    return EXP2_SCALE * lax.dot_general(
        keys, queries, (((1,), (1,)), ((), ())), preferred_element_type=jnp.float32
    )


def stage_kernel(plan, first, *refs):
    refs = list(refs)
    flags_ref = refs.pop(0)
    q_ref = refs.pop(0)
    inputs = [refs.pop(0) for _, count in plan for _ in range(count)]
    if not first:
        top_in, sum_in, acc_in = refs.pop(0), refs.pop(0), refs.pop(0)
    top_out, sum_out, acc_out = refs.pop(0), refs.pop(0), refs.pop(0)
    expo_out = refs.pop(0) if any(kind == "across" for kind, _ in plan) else None
    far_ref = refs.pop(0)
    bias_ref = refs.pop(0)
    tok = q_ref.shape[0]
    lower_core = flags_ref[0] == 0
    middle = flags_ref[2] != 0
    whole = []
    place = 0
    for kind, count in plan:
        parts = [inputs.pop(0) for _ in range(count)]
        if kind in ("own", "partner", "across"):
            whole.append((parts, kind))
        if kind == "partner":
            bias_ref[...] = triangle((tok, tok), lower_core)
        if kind == "across":
            valid = jnp.where(flags_ref[1] != 0, 0.0, NEG)
            bias_ref[...] = triangle((tok, tok), jnp.logical_not(lower_core)) + valid
        if kind in ("own", "across"):
            continue
        for side in range(2):
            at = place
            if kind == "partner":
                rows = pool_rows(parts[side][...])
            elif kind == "pick":
                rows = jnp.where(middle, parts[0][side], parts[1][side])
            else:
                rows = parts[0][side]
            far_ref[side, pl.ds(at, rows.shape[0]), :] = rows
            at += rows.shape[0]
            if kind != "far":
                lower = pool_rows(rows)
                far_ref[side, pl.ds(at, lower.shape[0]), :] = lower
                at += lower.shape[0]
        place = at
    cols = [pl.ds(head * HEAD_DIM, HEAD_DIM) for head in range(HEADS)]
    scores = []
    for head in range(HEADS):
        query = q_ref[:, cols[head]]
        pieces = []
        for parts, kind in whole:
            piece = key_scores(parts[0][:, cols[head]], query)
            pieces.append(piece if kind == "own" else piece + bias_ref[...])
        pieces.append(key_scores(far_ref[0, pl.ds(0, place), cols[head]], query))
        scores.append(pieces)
    highest, keep = [], []
    for head in range(HEADS):
        top = functools.reduce(
            jnp.maximum, [jnp.max(piece, axis=0, keepdims=True) for piece in scores[head]]
        )
        if not first:
            before = top_in[pl.ds(head, 1), :]
            top = jnp.maximum(top, before)
            keep.append(jnp.exp2(before - top))
        highest.append(top)
    expos, totals = [], []
    for head in range(HEADS):
        expos.append([jnp.exp2(piece - highest[head]) for piece in scores[head]])
        total = sum(jnp.sum(piece, axis=0, keepdims=True) for piece in expos[head])
        if not first:
            total = total + sum_in[pl.ds(head, 1), :] * keep[head]
        totals.append(total)
    for head in range(HEADS):
        mixed = 0.0
        for (parts, kind), expo in zip(whole, expos[head]):
            if kind == "across":
                expo_out[pl.ds(head * tok, tok), :] = expo.astype(jnp.bfloat16)
            else:
                mixed = mixed + weighted(parts[1][:, cols[head]], expo.astype(jnp.bfloat16))
        mixed = mixed + weighted(
            far_ref[1, pl.ds(0, place), cols[head]], expos[head][-1].astype(jnp.bfloat16)
        )
        if not first:
            mixed = mixed + acc_in[cols[head], :] * keep[head]
        acc_out[cols[head], :] = mixed
        top_out[pl.ds(head, 1), :] = highest[head]
        sum_out[pl.ds(head, 1), :] = totals[head]


def weighted(values, expo):
    return lax.dot_general(
        values, expo, (((0,), (0,)), ((), ())), preferred_element_type=jnp.float32
    )


def far_count(kind, parts):
    if kind in ("own", "across"):
        return 0
    if kind == "partner":
        rows = parts[0].shape[0] // POOL
    else:
        rows = parts[0].shape[1]
    return rows if kind == "far" else rows + rows // POOL


def stage(flags, queries, inputs, state=None):
    tok, width = queries.shape
    plan = [(kind, len(arrays)) for kind, *arrays in inputs]
    arrays = [array for _, *group in inputs for array in group]
    far = sum(far_count(kind, group) for kind, *group in inputs)
    near = tok * sum(kind in ("own", "partner", "across") for kind, *_ in inputs)
    vmem = pl.BlockSpec(memory_space=pltpu.VMEM)
    operands = [flags, queries, *arrays, *(state or ())]
    stat = jax.ShapeDtypeStruct((HEADS, tok), jnp.float32)
    out_shape = [stat, stat, jax.ShapeDtypeStruct((width, tok), jnp.float32)]
    if any(kind == "across" for kind, _ in plan):
        out_shape.append(jax.ShapeDtypeStruct((HEADS * tok, tok), jnp.bfloat16))
    return pl.pallas_call(
        functools.partial(stage_kernel, plan, state is None),
        out_shape=out_shape,
        in_specs=[pl.BlockSpec(memory_space=pltpu.SMEM)] + [vmem] * (len(operands) - 1),
        out_specs=[vmem] * len(out_shape),
        scratch_shapes=[
            pltpu.VMEM((2, far, width), jnp.bfloat16),
            pltpu.VMEM((tok, tok), jnp.float32),
        ],
        compiler_params=pltpu.CompilerParams(vmem_limit_bytes=VMEM_LIMIT),
        cost_estimate=pl.CostEstimate(
            flops=4 * tok * width * (far + near),
            bytes_accessed=sum(a.size * a.dtype.itemsize for a in operands),
            transcendentals=tok * HEADS * (far + near),
        ),
    )(*operands)


def finish_kernel(value_ref, expo_ref, before_ref, top_ref, sum_ref, acc_ref, out_ref, rows_ref, sem):
    tok = rows_ref.shape[0]
    width = rows_ref.shape[1] // OUT_PARTS
    copies = []
    for head in range(HEADS):
        cols = pl.ds(head * HEAD_DIM, HEAD_DIM)
        row = pl.ds(head, 1)
        keep = jnp.exp2(before_ref[row, :] - top_ref[row, :])
        mixed = weighted(value_ref[:, cols], expo_ref[pl.ds(head * tok, tok), :]) * keep
        mixed = (mixed + acc_ref[cols, :]) * (1.0 / sum_ref[row, :])
        rows_ref[:, cols] = mixed.T.astype(jnp.bfloat16)
        if (head + 1) * OUT_PARTS % HEADS == 0:
            part = (head + 1) * OUT_PARTS // HEADS - 1
            done = pl.ds(part * width, width)
            copies.append(
                pltpu.make_async_copy(rows_ref.at[:, done], out_ref.at[:, done], sem.at[part])
            )
            copies[-1].start()
    for copy in copies:
        copy.wait()


def finish(values, expo, before, top, total, mixed):
    tok, width = values.shape
    return pl.pallas_call(
        finish_kernel,
        out_shape=jax.ShapeDtypeStruct((tok, width), jnp.bfloat16),
        in_specs=[pl.BlockSpec(memory_space=pltpu.VMEM)] * 6,
        out_specs=pl.BlockSpec(memory_space=pltpu.HBM),
        scratch_shapes=[
            pltpu.VMEM((tok, width), jnp.bfloat16),
            pltpu.SemaphoreType.DMA((OUT_PARTS,)),
        ],
        name="finish",
        compiler_params=pltpu.CompilerParams(vmem_limit_bytes=VMEM_LIMIT),
        cost_estimate=pl.CostEstimate(
            flops=2 * tok * tok * width, bytes_accessed=10 * tok * width, transcendentals=0
        ),
    )(values, expo, before, top, total, mixed)


def swap(x, axis, mask):
    return lax.ppermute(x, axis, [(i, i ^ mask) for i in range(lax.axis_size(axis))])


def spread(x, axis, low, high):
    while low < high:
        x = jnp.concatenate([x, swap(x, axis, low)], axis=1)
        low *= 2
    return x


def pooled_means(stacked):
    count = stacked.shape[1] // POOL
    split = stacked.astype(jnp.float32).reshape(2, count, POOL, stacked.shape[2])
    return split.mean(axis=2).astype(jnp.bfloat16)


def attend(query_rows, key_rows, value_rows):
    tok = query_rows.shape[0]
    assert tok == HALF_WIN
    wide, tall = lax.axis_size("seqb"), lax.axis_size("seqa")
    count = tall * wide
    group = 2 * CHIPS_ONE
    inner = lax.axis_index("seqb")
    place = lax.axis_index("seqa") * wide + inner
    core = inner & 1
    valid = jnp.where(core == 0, place > 0, place < count - 1)
    chip = (inner >> 1) & (CHIPS_ONE - 1)
    middle = (chip == 1) | (chip == 2)
    flags = jnp.stack([flag.astype(jnp.int32) for flag in (core, valid, middle)])
    bounds = [(i, i + 1) for i in range(1, count - 1, 2)]
    bounds += [(j, i) for i, j in bounds]
    own_one, own_three = pool_call(key_rows, value_rows)

    one_far = swap(own_one, "seqb", group - 2)
    one_next = swap(own_one, "seqb", 2)
    other_three = swap(own_three, "seqb", 4)
    chips = [(i, i // 2 % CHIPS_ONE) for i in range(wide)]
    one_end = lax.ppermute(one_next, "seqb", [(i, i ^ 6) for i, chip in chips if chip in (1, 2)])
    across_keys = lax.ppermute(key_rows, AXES, bounds)
    across_values = lax.ppermute(value_rows, AXES, bounds)
    partner = [swap(key_rows, "seqb", 1), swap(value_rows, "seqb", 1)]
    near_plan = [("own", key_rows, value_rows), ("one", own_one), ("partner", *partner)]
    state = stage(flags, query_rows, near_plan)
    one_mid = lax.ppermute(one_far, "seqb", [(i, i ^ 2) for i, chip in chips if chip in (1, 2)])
    three = lift_call(own_three, other_three, one_next, one_far)
    three = spread(three, "seqb", group, wide)
    three = spread(three, "seqa", 1, COLUMNS_THREE)
    far = [
        ("one", one_next),
        ("one", swap(one_next, "seqb", 1)),
        ("one", one_far),
        ("one", swap(one_far, "seqb", 1)),
    ]
    state = stage(flags, query_rows, far, state)
    third = [
        ("pick", one_end, one_mid),
        ("pick", swap(one_end, "seqb", 1), swap(one_mid, "seqb", 1)),
    ]
    wider = [
        ("three", three),
        ("three", swap(three, "seqb", 1)),
    ]
    if wide > group:
        two = pooled_means(own_one)
        others = spread(two, "seqb", group, wide)[:, two.shape[1] :]
        wider.append(("far", spread(others, "seqb", 1, group)))
    if tall > COLUMNS_THREE:
        four = pooled_means(own_three)
        others = spread(four, "seqa", COLUMNS_THREE, tall)[:, four.shape[1] :]
        others = spread(others, "seqa", 1, COLUMNS_THREE)
        wider.append(("far", spread(others, "seqb", 1, wide)))
    *state, expo = stage(flags, query_rows, wider + [("across", across_keys)], state)
    top, total, mixed = stage(flags, query_rows, third, state)
    return finish(across_values, expo, state[0], top, total, mixed)


def solution(mesh):
    return jax.shard_map(
        attend,
        mesh=mesh,
        in_specs=(P(AXES, None), P(AXES, None), P(AXES, None)),
        out_specs=P(AXES, None),
        check_vma=False,
    )
```
